512 devices in a mesh: row: 16 (over z, core), col: 32 (over y, x).
Axes of the slice: x: 4, y: 8, z: 8, core: 2. Of those that a mesh axis runs over, the one named last changes fastest.
Arguments:
- block: float32 [8192, 4096], P('row', 'col'), may hold values from -6 to 6
- panels: float32 [2, 8192, 256], P(None, 'row', 'col'), may hold values from -0.125 to 0.125
- pivots: int32 [2, 256], replicated, may hold values from 0 to 8191, as said below
Outputs:
- updated: float32 [8192, 4096], P('row', 'col')
The draws below stay inside these ranges and needn't reach their ends.
Inputs may be any that keep to these rules, and one draw needn't show every extreme that they name: `pivots`: entry j of list k is either k*256+j itself or a global row at or beyond (k+1)*256; within one list the entries beyond are all different; entry 0 of list 0 is 0 and entry 255 of list 0 is 8191.
All inputs are finite; a program needn't handle non-finite values.
Results may differ from the reference program's by a relative error of at most 0.0001.
Values sent between devices are 32-bit elements; how exact they have to be, the bound alone decides.
No kernel may reach another device: no remote copies, remote signals or barrier semaphores. Data moves between devices by JAX's collectives and lax.ppermute only.
A program may use at most 64 MiB of HBM per device.

```python
import jax
import jax.numpy as jnp
from jax import lax

PW = 256
ROWS = 8192
COLS = 4096


def draw_pivots(key, part):
    lists = []
    for panel in range(2):
        offset = panel * PW
        own = offset + jnp.arange(PW, dtype=jnp.int32)
        span = ROWS - 1 - (offset + PW)
        chosen = jax.random.permutation(jax.random.fold_in(key, 31 + panel), span)[:PW].astype(jnp.int32) + offset + PW
        keep = jax.random.randint(jax.random.fold_in(key, 57 + panel), (PW,), 0, 4) == 0
        entry = jnp.where(keep, own, chosen)
        if panel == 0:
            entry = entry.at[0].set(0).at[PW - 1].set(ROWS - 1)
        lists.append(entry.astype(jnp.int32))
    return jnp.stack(lists).astype(jnp.int32)


def shard_levels(own_key, dims, shards, smallest, largest):
    gain = 1.0
    for position, blocks in shards:
        steps = jax.random.uniform(jax.random.fold_in(jax.random.fold_in(own_key, 6), position), (blocks,), jnp.float32, smallest / len(shards), largest / len(shards))
        gain = gain * jnp.repeat(jnp.exp(steps), dims[position] // blocks).reshape((-1,) + (1,) * (len(dims) - 1 - position))
    return gain


def gaussian(stream_key, extent, spread, bound, cuts=(), held_as=jnp.bfloat16):
    array = spread * jax.random.normal(stream_key, extent, jnp.float32)
    if cuts:
        array = array * shard_levels(stream_key, extent, cuts, -0.22, 0.18)
    return jnp.clip(array, -bound, bound).astype(held_as)


def setup_inputs(seed: int = 0) -> dict:
    seeds = jax.random.split(jax.random.key(seed), 4)
    block = gaussian(seeds[0], (ROWS, COLS), 1.0, 6.0, ((0, 16), (1, 32)), jnp.float32)
    panels = gaussian(seeds[1], (2, ROWS, PW), (8 * PW) ** -0.5, 0.125, ((1, 16), (2, 32)), jnp.float32)
    pivots = draw_pivots(jax.random.fold_in(seeds[3], 71), 0)
    return dict(block=block, panels=panels, pivots=pivots)


def swap_order(piv_row, offset, count):

    def step(j, perm):
        first = offset + j
        second = piv_row[j]
        value_a = perm[first]
        value_b = perm[second]
        return perm.at[first].set(value_b).at[second].set(value_a)
    return lax.fori_loop(0, piv_row.shape[0], step, jnp.arange(count, dtype=jnp.int32))

def reference(block, panels, pivots):
    work = block
    for panel in range(2):
        offset = panel * PW
        perm = swap_order(pivots[panel], offset, ROWS)
        work = work[perm]
        lower = panels[panel]
        diag = jnp.tril(lower[offset:offset + PW], -1) + jnp.eye(PW, dtype=jnp.float32)
        upper = lax.linalg.triangular_solve(diag, work[offset:offset + PW], left_side=True, lower=True, unit_diagonal=True)
        below = work[offset + PW:] - jnp.dot(lower[offset + PW:].astype(jnp.float32), upper.astype(jnp.float32), precision=lax.Precision.HIGHEST, preferred_element_type=jnp.float32)
        work = jnp.concatenate([work[:offset], upper, below], 0)
    return work
```

```python
import jax
import jax.numpy as jnp
from jax import lax
from jax.sharding import PartitionSpec as P

PW = 256
NZ, NC = 8, 2
NY, NX = 8, 4
Z_GROUPS = [[NC * z + core for z in range(NZ)] for core in range(NC)]
X_GROUPS = [[NX * y + x for x in range(NX)] for y in range(NY)]
Y_GROUPS = [[NX * y + x for y in range(NY)] for x in range(NX)]
PAIR = [(i, i ^ 1) for i in range(NZ * NC)]


def mm(a, b, ca=1, cb=0):
    return lax.dot_general(
        a, b, (((ca,), (cb,)), ((), ())),
        precision=lax.Precision.HIGHEST, preferred_element_type=jnp.float32,
    )


def spread(x, axis, groups):
    n = len(groups[0])
    return lax.all_to_all(
        jnp.broadcast_to(x[None], (n,) + x.shape), axis, 0, 0, tiled=True, axis_index_groups=groups
    )


def invert_t(diag_t):
    strict = jnp.triu(diag_t, 1)
    inverse = jnp.eye(PW, dtype=jnp.float32) - strict
    power = strict
    for _ in range(1, PW.bit_length() - 1):
        power = mm(power, power)
        inverse = inverse + mm(inverse, power)
    return inverse


def body(block, panels, pivots):
    me = lax.axis_index("row")
    core = me % NC
    start = me * 512
    first = me == 0
    p0, p1 = pivots[0], pivots[1]
    j = jnp.arange(PW, dtype=jnp.int32)
    lane = jnp.arange(512, dtype=jnp.int32)

    def through0(rows):
        hit = p0[None, :] == rows[:, None]
        found = jnp.max(jnp.where(hit, j[None, :], -1), axis=1)
        return jnp.where(found >= 0, found, rows)

    source = jnp.concatenate([p0, through0(p1), j, through0(PW + j)])
    pick = (source[:, None] - start == lane[None, :]).astype(jnp.float32)
    rows = mm(pick, block).reshape(2, NC, NZ, 32, 128)
    rows = rows.transpose(1, 2, 0, 3, 4).reshape(NC, NZ, 64, 128)

    pan_t = panels.transpose(0, 2, 1)
    at1 = (p1[:, None] - start == lane[None, :]).astype(jnp.float32)
    piv_t = mm(pan_t[0], at1, 1, 1)
    zero = jnp.zeros((8, PW), jnp.float32)
    own = lambda t: jnp.where(first, t, zero)
    pieces = jnp.stack([own(pan_t[0, :, :PW]), own(pan_t[1, :, PW:]), own(pan_t[0, :, PW:]), piv_t])
    tiles = pieces.reshape(4, 8, 2, 128).transpose(0, 2, 1, 3).reshape(8, 8, 128)

    mine = jnp.where(core == 0, rows[0], rows[1])
    other = jnp.where(core == 0, rows[1], rows[0])
    got = lax.ppermute(jnp.concatenate([other, tiles], 1), "row", PAIR)
    part = jnp.concatenate([mine, tiles], 1) + got
    part = lax.all_to_all(part, "row", 0, 0, tiled=True, axis_index_groups=Z_GROUPS)
    part = jnp.sum(part, 0)

    own_tiles = pan_t.reshape(2, 8, 4, 128).transpose(0, 2, 1, 3).reshape(64, 128)
    sent = jnp.concatenate([own_tiles, part[64:]], 0)
    sent = spread(sent, "col", Y_GROUPS)
    sent = spread(sent, "col", X_GROUPS)
    lower_t = sent[:, :, :64].reshape(NX, NY, 2, 4, 8, 128).transpose(2, 1, 0, 4, 3, 5).reshape(2, PW, 512)
    tile = sent[:, :, 64:]
    half = jnp.where(core == 0, tile[:2], tile[2:]).reshape(128, 128)

    wide = spread(jnp.concatenate([part[:64], half], 0), "row", Z_GROUPS)
    got = lax.ppermute(wide, "row", PAIR)
    low = jnp.where(core == 0, wide, got)
    high = jnp.where(core == 0, got, wide)
    both = jnp.stack([low, high])
    top = both[:, :, :32].reshape(512, 128)
    moved = both[:, :, 32:64].reshape(512, 128)
    square = both[:, :, 64:].reshape(NC, 4, 2, 2, NY, 8, 128)
    square = square.transpose(1, 4, 0, 3, 5, 2, 6).reshape(4, PW, PW)

    upper0 = mm(invert_t(square[0]), top[:PW], 0, 0)
    upper1 = mm(invert_t(square[1]), top[PW:] - mm(square[3], upper0, 0, 0), 0, 0)
    second = moved[PW:] - mm(square[2], upper0, 0, 0)

    at0 = (p0[:, None] - start == lane[None, :]).astype(jnp.float32)
    in0 = jnp.sum(at0, 0)[:, None] > 0
    in1 = jnp.sum(at1, 0)[:, None] > 0
    work = jnp.where(in0, mm(at0, moved[:PW], 0, 0), block) - mm(lower_t[0], upper0, 0, 0)
    work = jnp.where(in1, mm(at1, second, 0, 0), work) - mm(lower_t[1], upper1, 0, 0)
    return jnp.where(first, jnp.concatenate([upper0, upper1], 0), work)


def solution(mesh):
    return jax.shard_map(
        body,
        mesh=mesh,
        in_specs=(P("row", "col"), P(None, "row", "col"), P()),
        out_specs=P("row", "col"),
        check_vma=False,
    )
```

```python
import jax
import jax.numpy as jnp
from jax import lax
from jax.sharding import PartitionSpec as P

PW = 256
NZ, NC = 8, 2
NY, NX = 8, 4
Z_GROUPS = [[NC * z + core for z in range(NZ)] for core in range(NC)]
ORDER = [0]
for step in (4, 8, 16, 1, 2):
    ORDER = ORDER + [i ^ step for i in ORDER]
PAIR = [(i, i ^ 1) for i in range(NZ * NC)]


def mm(a, b, ca=1, cb=0):
    return lax.dot_general(
        a, b, (((ca,), (cb,)), ((), ())),
        precision=lax.Precision.HIGHEST, preferred_element_type=jnp.float32,
    )


def spread(x, axis, groups):
    n = len(groups[0])
    return lax.all_to_all(
        jnp.broadcast_to(x[None], (n,) + x.shape), axis, 0, 0, tiled=True, axis_index_groups=groups
    )


def double(x, step):
    pairs = [(i, i ^ step) for i in range(NX * NY)]
    return jnp.concatenate([x, lax.ppermute(x, "col", pairs)], 0)


def invert_t(diag_t):
    strict = jnp.triu(diag_t, 1)
    inverse = jnp.eye(PW, dtype=jnp.float32) - strict
    power = strict
    for _ in range(1, PW.bit_length() - 1):
        power = mm(power, power)
        inverse = inverse + mm(inverse, power)
    return inverse


def body(block, panels, pivots):
    me = lax.axis_index("row")
    core = me % NC
    start = me * 512
    first = me == 0
    p0, p1 = pivots[0], pivots[1]
    j = jnp.arange(PW, dtype=jnp.int32)
    lane = jnp.arange(512, dtype=jnp.int32)

    def through0(rows):
        hit = p0[None, :] == rows[:, None]
        found = jnp.max(jnp.where(hit, j[None, :], -1), axis=1)
        return jnp.where(found >= 0, found, rows)

    source = jnp.concatenate([p0, through0(p1), j, through0(PW + j)])
    pick = (source[:, None] - start == lane[None, :]).astype(jnp.float32)
    rows = mm(pick, block).reshape(2, NC, NZ, 32, 128)
    rows = rows.transpose(1, 2, 0, 3, 4).reshape(NC, NZ, 64, 128)

    pan_t = panels.transpose(0, 2, 1)
    at1 = (p1[:, None] - start == lane[None, :]).astype(jnp.float32)
    piv_t = mm(pan_t[0], at1, 1, 1)
    zero = jnp.zeros((8, PW), jnp.float32)
    own = lambda t: jnp.where(first, t, zero)
    pieces = jnp.stack([own(pan_t[0, :, :PW]), own(pan_t[1, :, PW:]), own(pan_t[0, :, PW:]), piv_t])
    tiles = pieces.reshape(4, 8, 2, 128).transpose(0, 2, 1, 3).reshape(8, 8, 128)

    mine = jnp.where(core == 0, rows[0], rows[1])
    other = jnp.where(core == 0, rows[1], rows[0])
    got = lax.ppermute(jnp.concatenate([other, tiles], 1), "row", PAIR)
    part = jnp.concatenate([mine, tiles], 1) + got
    near = pan_t.reshape(2, 8, 4, 128).transpose(0, 2, 1, 3).reshape(1, 64, 128)

    part, near = lax.optimization_barrier((part, near))
    part = lax.all_to_all(part, "row", 0, 0, tiled=True, axis_index_groups=Z_GROUPS)
    near = double(near, 4)
    near = double(near, 8)
    part, near = lax.optimization_barrier((part, near))

    part = jnp.sum(part, 0)
    tile = lax.all_to_all(jnp.broadcast_to(part[64:], (NX * NY, 8, 128)), "col", 0, 0, tiled=True)
    near = double(near, 16)
    tile, near = lax.optimization_barrier((tile, near))

    half = jnp.where(core == 0, tile[:16], tile[16:]).reshape(128, 128)
    wide = spread(jnp.concatenate([part[:64], half], 0), "row", Z_GROUPS)
    near = double(near, 1)
    near = double(near, 2)
    wide, near = lax.optimization_barrier((wide, near))

    got = lax.ppermute(wide, "row", PAIR)
    low = jnp.where(core == 0, wide, got)
    high = jnp.where(core == 0, got, wide)
    both = jnp.stack([low, high])
    top = both[:, :, :32].reshape(512, 128)
    moved = both[:, :, 32:64].reshape(512, 128)
    square = both[:, :, 64:].reshape(NC, 4, 2, 16, 8, 128)
    square = square.transpose(1, 0, 3, 4, 2, 5).reshape(4, PW, PW)
    lower_t = near.reshape(32, 2, 4, 8, 128).transpose(1, 0, 3, 2, 4).reshape(2, PW, 512)
    seen = lax.axis_index("col") ^ jnp.array(ORDER, jnp.int32)

    upper0 = mm(invert_t(square[0]), top[:PW], 0, 0)
    upper1 = mm(invert_t(square[1]), top[PW:] - mm(square[3], upper0, 0, 0), 0, 0)
    second = moved[PW:] - mm(square[2], upper0, 0, 0)

    at0 = (p0[:, None] - start == lane[None, :]).astype(jnp.float32)
    in0 = jnp.sum(at0, 0)[:, None] > 0
    in1 = jnp.sum(at1, 0)[:, None] > 0
    work = jnp.where(in0, mm(at0, moved[:PW], 0, 0), block) - mm(lower_t[0], upper0.reshape(32, 8, 128)[seen].reshape(PW, 128), 0, 0)
    work = jnp.where(in1, mm(at1, second, 0, 0), work) - mm(lower_t[1], upper1.reshape(32, 8, 128)[seen].reshape(PW, 128), 0, 0)
    return jnp.where(first, jnp.concatenate([upper0, upper1], 0), work)


def solution(mesh):
    return jax.shard_map(
        body,
        mesh=mesh,
        in_specs=(P("row", "col"), P(None, "row", "col"), P()),
        out_specs=P("row", "col"),
        check_vma=False,
    )
```

```python
import jax
import jax.numpy as jnp
from jax import lax
from jax.sharding import PartitionSpec as P


PW = 256
NZ, NC = 8, 2
NY, NX = 8, 4
Z_GROUPS = [[NC * z + core for z in range(NZ)] for core in range(NC)]
Y_GROUPS = [[NX * y + x for y in range(NY)] for x in range(NX)]
PAIR = [(i, i ^ 1) for i in range(NZ * NC)]


def mm(a, b, ca=1, cb=0):
    return lax.dot_general(
        a, b, (((ca,), (cb,)), ((), ())),
        precision=lax.Precision.HIGH, preferred_element_type=jnp.float32,
    )


def spread(x, axis, groups):
    n = len(groups[0])
    return lax.all_to_all(
        jnp.broadcast_to(x[None], (n,) + x.shape), axis, 0, 0, tiled=True, axis_index_groups=groups
    )


def double(x, step):
    pairs = [(i, i ^ step) for i in range(NX * NY)]
    return jnp.concatenate([x, lax.ppermute(x, "col", pairs)], 0)


def join(core, own, got):
    return jnp.stack([jnp.where(core == 0, own, got), jnp.where(core == 0, got, own)])


def invert_t(diag_t):
    strict = jnp.triu(diag_t, 1)
    inverse = jnp.eye(PW, dtype=jnp.float32) - strict
    power = strict
    for _ in range(1, PW.bit_length() - 1):
        power = mm(power, power)
        inverse = inverse + mm(inverse, power)
    return inverse


def step(block, panels, pivots):
    me = lax.axis_index("row")
    core = me % NC
    start = me * 512
    first = me == 0
    p0, p1 = pivots[0], pivots[1]
    j = jnp.arange(PW, dtype=jnp.int32)
    lane = jnp.arange(512, dtype=jnp.int32)

    def through0(rows):
        hit = p0[None, :] == rows[:, None]
        found = jnp.max(jnp.where(hit, j[None, :], -1), axis=1)
        return jnp.where(found >= 0, found, rows)

    source = jnp.concatenate([p0, through0(p1), j, through0(PW + j)])
    pick = (source[:, None] - start == lane[None, :]).astype(jnp.float32)
    rows = mm(pick, block).reshape(2, NC, NZ, 32, 128)
    rows = rows.transpose(1, 2, 0, 3, 4).reshape(NC, NZ, 64, 128)

    pan_t = panels.transpose(0, 2, 1)
    near = pan_t.reshape(2, 8, 4, 128).transpose(0, 2, 1, 3).reshape(64, 128)
    near = spread(near, "col", Y_GROUPS)

    at1 = (p1[:, None] - start == lane[None, :]).astype(jnp.float32)
    piv_t = mm(pan_t[0], at1, 1, 1)
    zero = jnp.zeros((8, PW), jnp.float32)
    own = lambda t: jnp.where(first, t, zero)
    pieces = jnp.stack([own(pan_t[0, :, :PW]), own(pan_t[1, :, PW:]), own(pan_t[0, :, PW:]), piv_t])
    tiles = pieces.reshape(4, 8, 2, 128).transpose(2, 0, 1, 3).reshape(2, 32, 128)

    def side(pair, mine):
        return jnp.where((core == 0) == mine, pair[0], pair[1])

    def halves(mine):
        return jnp.concatenate([side(rows, mine).reshape(512, 128), side(tiles, mine)], 0)

    part = halves(True) + lax.ppermute(halves(False), "row", PAIR)
    part = jnp.concatenate(
        [part[:512].reshape(NZ, 64, 128), jnp.broadcast_to(part[None, 512:], (NZ, 32, 128))], 1
    )
    part, near = lax.optimization_barrier((part, near))

    part = lax.all_to_all(part, "row", 0, 0, tiled=True, axis_index_groups=Z_GROUPS)
    near = double(near, 1)
    part, near = lax.optimization_barrier((part, near))

    part = jnp.sum(part, 0)
    tile = lax.all_to_all(jnp.broadcast_to(part[64:], (NX * NY, 32, 128)), "col", 0, 0, tiled=True)
    near = double(near, 2)
    tile, part, near = lax.optimization_barrier((tile, part, near))

    wide = spread(part[:64], "row", Z_GROUPS)
    far = lax.ppermute(tile, "row", PAIR)
    square = join(core, tile, far).reshape(NC, 32, 4, 8, 128)
    square = square.transpose(2, 1, 3, 0, 4).reshape(4, PW, PW)
    inverse0 = invert_t(square[0])
    inverse1 = invert_t(square[1])
    wide, inverse0, inverse1 = lax.optimization_barrier((wide, inverse0, inverse1))

    both = join(core, wide, lax.ppermute(wide, "row", PAIR))
    top = both[:, :, :32].reshape(512, 128)
    moved = both[:, :, 32:].reshape(512, 128)
    lower_t = near.reshape(32, 2, 4, 8, 128).transpose(1, 0, 3, 2, 4).reshape(2, PW, 512)
    x_at = lax.axis_index("col") % NX
    seen = jnp.concatenate([NX * jnp.arange(NY, dtype=jnp.int32) + (x_at ^ b) for b in range(NX)])

    upper0 = mm(inverse0, top[:PW], 0, 0)
    upper1 = mm(inverse1, top[PW:] - mm(square[3], upper0, 0, 0), 0, 0)
    second = moved[PW:] - mm(square[2], upper0, 0, 0)

    at0 = (p0[:, None] - start == lane[None, :]).astype(jnp.float32)
    in0 = jnp.sum(at0, 0)[:, None] > 0
    in1 = jnp.sum(at1, 0)[:, None] > 0
    work = jnp.where(in0, mm(at0, moved[:PW], 0, 0), block) - mm(lower_t[0], upper0.reshape(32, 8, 128)[seen].reshape(PW, 128), 0, 0)
    work = jnp.where(in1, mm(at1, second, 0, 0), work) - mm(lower_t[1], upper1.reshape(32, 8, 128)[seen].reshape(PW, 128), 0, 0)
    return jnp.where(first, jnp.concatenate([upper0, upper1], 0), work)


def solution(mesh):
    return jax.shard_map(
        step,
        mesh=mesh,
        in_specs=(P("row", "col"), P(None, "row", "col"), P()),
        out_specs=P("row", "col"),
        check_vma=False,
    )
```

```python
import jax
import jax.numpy as jnp
from jax import lax
from jax.experimental import pallas as pl
from jax.experimental.pallas import tpu as pltpu
from jax.sharding import PartitionSpec as P


PW = 256
LIMIT = 16 << 20
NZ, NC = 8, 2
NY, NX = 8, 4
Z_GROUPS = [[NC * z + core for z in range(NZ)] for core in range(NC)]
Y_GROUPS = [[NX * y + x for y in range(NY)] for x in range(NX)]
PAIR = [(i, i ^ 1) for i in range(NZ * NC)]


def mm(a, b, ca=1, cb=0):
    return lax.dot_general(
        a, b, (((ca,), (cb,)), ((), ())),
        precision=lax.Precision.HIGH, preferred_element_type=jnp.float32,
    )


def spread(x, axis, groups):
    n = len(groups[0])
    return lax.all_to_all(
        jnp.broadcast_to(x[None], (n,) + x.shape), axis, 0, 0, tiled=True, axis_index_groups=groups
    )


def flip(x, bits):
    return lax.ppermute(x, "col", [(i, i ^ bits) for i in range(NX * NY)])


def split(x):
    high = x.astype(jnp.bfloat16)
    return high, (x - high.astype(jnp.float32)).astype(jnp.bfloat16)


def dot(a, b):
    return jnp.dot(a, b, preferred_element_type=jnp.float32)


def dot3(a, b):
    return dot(a[0], b[0]) + dot(a[0], b[1]) + dot(a[1], b[0])


def halves_of(core, own, far):
    return jnp.where(core == 0, own, far), jnp.where(core == 0, far, own)


def squares_kernel(core_ref, own_ref, far_ref, high_ref, low_ref):
    core = core_ref[0]
    squares = []
    for p in range(4):
        own = own_ref[:, 8 * p : 8 * p + 8, :].reshape(PW, 128)
        far = far_ref[:, 8 * p : 8 * p + 8, :].reshape(PW, 128)
        squares.append(jnp.concatenate(halves_of(core, own, far), 1).T)
    row = lax.broadcasted_iota(jnp.int32, (PW, PW), 0)
    col = lax.broadcasted_iota(jnp.int32, (PW, PW), 1)
    eye = (row == col).astype(jnp.float32)
    power = [split(jnp.where(row > col, x, 0.0)) for x in squares[:2]]
    inverse = [eye - jnp.where(row > col, x, 0.0) for x in squares[:2]]
    for _ in range(1, PW.bit_length() - 1):
        power = [split(dot3(x, x)) for x in power]
        inverse = [x + dot3(split(x), y) for x, y in zip(inverse, power)]
    for p, x in enumerate(inverse + squares[2:]):
        high, low = split(x)
        high_ref[p] = high
        low_ref[p] = low


def squares_of(core, own, far):
    vmem = pl.BlockSpec(memory_space=pltpu.VMEM)
    pair = jax.ShapeDtypeStruct((4, PW, PW), jnp.bfloat16)
    return pl.pallas_call(
        squares_kernel,
        out_shape=(pair, pair),
        in_specs=[pl.BlockSpec(memory_space=pltpu.SMEM), vmem, vmem],
        out_specs=(vmem, vmem),
        cost_estimate=pl.CostEstimate(flops=6 * 28 * PW**3, bytes_accessed=2 << 20, transcendentals=0),
        compiler_params=pltpu.CompilerParams(vmem_limit_bytes=LIMIT),
        name="squares",
    )(core, own, far)


def lower_kernel(col_ref, near0_ref, near1_ref, near2_ref, near3_ref, high_ref, low_ref, turned_ref):
    x_at = col_ref[0] % NX
    for bits, ref in enumerate((near0_ref, near1_ref, near2_ref, near3_ref)):
        x = x_at ^ bits
        for y in range(NY):
            at = pl.multiple_of((NX * y + x) * 8, 8)
            for p in range(2):
                for h in range(4):
                    tile = ref[y, 32 * p + 8 * h : 32 * p + 8 * h + 8, :]
                    turned_ref[p, pl.ds(at, 8), 128 * h : 128 * h + 128] = tile

    for p in range(2):
        high, low = split(turned_ref[p].T)
        high_ref[p] = high
        low_ref[p] = low


def lower_of(col, *near):
    vmem = pl.BlockSpec(memory_space=pltpu.VMEM)
    pair = jax.ShapeDtypeStruct((2, 512, PW), jnp.bfloat16)
    return pl.pallas_call(
        lower_kernel,
        out_shape=(pair, pair),
        in_specs=[pl.BlockSpec(memory_space=pltpu.SMEM)] + [vmem] * 4,
        out_specs=(vmem, vmem),
        scratch_shapes=[pltpu.VMEM((2, PW, 512), jnp.float32)],
        cost_estimate=pl.CostEstimate(flops=1 << 20, bytes_accessed=2 << 20, transcendentals=0),
        compiler_params=pltpu.CompilerParams(vmem_limit_bytes=LIMIT),
        name="lower",
    )(col, *near)


def update_kernel(me_ref, piv_ref, wide_ref, sq_high_ref, sq_low_ref, lo_high_ref, lo_low_ref, block_ref, out_ref):
    me = me_ref[0]
    start = me * 512

    def rows(at):
        return wide_ref[:, at : at + 32, :].reshape(PW, 128)

    square = [(sq_high_ref[p], sq_low_ref[p]) for p in range(4)]
    upper0 = dot3(square[0], split(rows(0)))
    pair0 = split(upper0)
    upper1 = dot3(square[1], split(rows(64) - dot3(square[3], pair0)))

    @pl.when(me == 0)
    def _():
        out_ref[:PW] = upper0
        out_ref[PW:] = upper1

    @pl.when(me != 0)
    def _():
        second = rows(96) - dot3(square[2], pair0)
        at = lax.broadcasted_iota(jnp.int32, (512, PW), 0) + start

        def place(p, x, work):
            select = (at == piv_ref[p : p + 1, :]).astype(jnp.bfloat16)
            high = x.astype(jnp.bfloat16)
            rest = x - high.astype(jnp.float32)
            mid = rest.astype(jnp.bfloat16)
            low = (rest - mid.astype(jnp.float32)).astype(jnp.bfloat16)
            one = dot(select, jnp.concatenate([high, jnp.ones((PW, 128), jnp.bfloat16)], 1))
            two = dot(select, jnp.concatenate([mid, low], 1))
            moved = one[:, :128] + two[:, :128] + two[:, 128:]
            return jnp.where(one[:, 128:] > 0, moved, work)

        work = place(0, rows(32), block_ref[...])
        work = work - dot3((lo_high_ref[0], lo_low_ref[0]), pair0)
        work = place(1, second, work)
        out_ref[...] = work - dot3((lo_high_ref[1], lo_low_ref[1]), split(upper1))


def update_of(me, pivots, wide, squares, lower, block):
    vmem = pl.BlockSpec(memory_space=pltpu.VMEM)
    return pl.pallas_call(
        update_kernel,
        out_shape=jax.ShapeDtypeStruct((512, 128), jnp.float32),
        in_specs=[pl.BlockSpec(memory_space=pltpu.SMEM)] + [vmem] * 7,
        out_specs=vmem,
        cost_estimate=pl.CostEstimate(flops=1 << 29, bytes_accessed=3 << 20, transcendentals=0),
        compiler_params=pltpu.CompilerParams(vmem_limit_bytes=LIMIT),
        name="update",
    )(me, pivots, wide, *squares, *lower, block)


def step(block, panels, pivots):
    me = lax.axis_index("row")
    core = me % NC
    start = me * 512
    first = me == 0
    p0, p1 = pivots[0], pivots[1]
    j = jnp.arange(PW, dtype=jnp.int32)
    lane = jnp.arange(512, dtype=jnp.int32)

    def through0(rows):
        hit = p0[None, :] == rows[:, None]
        found = jnp.max(jnp.where(hit, j[None, :], -1), axis=1)
        return jnp.where(found >= 0, found, rows)

    source = jnp.concatenate([p0, through0(p1), j, through0(PW + j)])
    pick = (source[:, None] - start == lane[None, :]).astype(jnp.float32)
    rows = mm(pick, block).reshape(2, NC, NZ, 32, 128)
    rows = rows.transpose(1, 2, 0, 3, 4).reshape(NC, NZ, 64, 128)

    pan_t = panels.transpose(0, 2, 1)
    near = pan_t.reshape(2, 8, 4, 128).transpose(0, 2, 1, 3).reshape(64, 128)
    near = spread(near, "col", Y_GROUPS)

    at1 = (p1[:, None] - start == lane[None, :]).astype(jnp.float32)
    piv_t = mm(pan_t[0], at1, 1, 1)
    zero = jnp.zeros((8, PW), jnp.float32)
    own = lambda t: jnp.where(first, t, zero)
    pieces = jnp.stack([own(pan_t[0, :, :PW]), own(pan_t[1, :, PW:]), own(pan_t[0, :, PW:]), piv_t])
    tiles = pieces.reshape(4, 8, 2, 128).transpose(2, 0, 1, 3).reshape(2, 32, 128)

    def side(pair, mine):
        return jnp.where((core == 0) == mine, pair[0], pair[1])

    def halves(mine):
        return jnp.concatenate([side(rows, mine).reshape(512, 128), side(tiles, mine)], 0)

    part = halves(True) + lax.ppermute(halves(False), "row", PAIR)
    part = jnp.concatenate(
        [part[:512].reshape(NZ, 64, 128), jnp.broadcast_to(part[None, 512:], (NZ, 32, 128))], 1
    )
    part, near = lax.optimization_barrier((part, near))

    part = lax.all_to_all(part, "row", 0, 0, tiled=True, axis_index_groups=Z_GROUPS)
    near1 = flip(near, 1)
    part, near, near1 = lax.optimization_barrier((part, near, near1))

    part = jnp.sum(part, 0)
    tile = jnp.broadcast_to(part[64:], (NX * NY, 32, 128))
    tile = lax.all_to_all(tile, "col", 0, 0, tiled=True)
    near2 = flip(near, 2)
    far = lax.ppermute(part[:64], "row", PAIR)
    both = jnp.where(core == 0, jnp.concatenate([part[:64], far]), jnp.concatenate([far, part[:64]]))
    tile, both, near2 = lax.optimization_barrier((tile, both, near2))

    wide = spread(both, "row", Z_GROUPS)
    far = lax.ppermute(tile, "row", PAIR)
    near3 = flip(near, 3)
    squares = squares_of(core.reshape(1), tile, far)
    lower = lower_of(lax.axis_index("col").reshape(1), near, near1, near2, near3)
    wide, squares, lower = lax.optimization_barrier((wide, squares, lower))
    return update_of(me.reshape(1), pivots, wide, squares, lower, block)


def solution(mesh):
    return jax.shard_map(
        step,
        mesh=mesh,
        in_specs=(P("row", "col"), P(None, "row", "col"), P()),
        out_specs=P("row", "col"),
        check_vma=False,
    )
```

```python
import jax
import jax.numpy as jnp
from jax import lax
from jax.experimental import pallas as pl
from jax.experimental.pallas import tpu as pltpu
from jax.sharding import PartitionSpec as P


PW = 256
LIMIT = 16 << 20
NZ, NC = 8, 2
NY, NX = 8, 4
TURN = [0, 4, 1, 5, 2, 6, 3, 7]
Z_GROUPS = [[NC * z + core for z in TURN] for core in range(NC)]
Y_GROUPS = [[NX * y + x for y in TURN] for x in range(NX)]
COL_GROUPS = [[NX * y + x for x in range(NX) for y in TURN]]
PAIR = [(i, i ^ 1) for i in range(NZ * NC)]


def mm(a, b, ca=1, cb=0):
    return lax.dot_general(
        a, b, (((ca,), (cb,)), ((), ())),
        precision=lax.Precision.HIGH, preferred_element_type=jnp.float32,
    )


def spread(x, axis, groups):
    n = len(groups[0])
    return lax.all_to_all(
        jnp.broadcast_to(x[None], (n,) + x.shape), axis, 0, 0, tiled=True, axis_index_groups=groups
    )


def flip(x, bits):
    return lax.ppermute(x, "col", [(i, i ^ bits) for i in range(NX * NY)])


def split(x):
    high = x.astype(jnp.bfloat16)
    return high, (x - high.astype(jnp.float32)).astype(jnp.bfloat16)


def dot(a, b):
    return jnp.dot(a, b, preferred_element_type=jnp.float32)


def dot3(a, b):
    return dot(a[0], b[0]) + dot(a[0], b[1]) + dot(a[1], b[0])


def dot3_narrow(a, b):
    both = dot(a[0], jnp.concatenate(b, 1))
    return both[:, :128] + both[:, 128:] + dot(a[1], b[0])


def halves_of(core, own, far):
    return jnp.where(core == 0, own, far), jnp.where(core == 0, far, own)


def squares_kernel(core_ref, own_ref, far_ref, high_ref, low_ref):
    core = core_ref[0]
    squares = []
    for p in range(4):
        order = [COL_GROUPS[0].index(c) for c in range(NX * NY)]
        own = jnp.concatenate([own_ref[i, 8 * p : 8 * p + 8, :] for i in order], 0)
        far = jnp.concatenate([far_ref[i, 8 * p : 8 * p + 8, :] for i in order], 0)
        squares.append(jnp.concatenate(halves_of(core, own, far), 1).T)
    row = lax.broadcasted_iota(jnp.int32, (PW, PW), 0)
    col = lax.broadcasted_iota(jnp.int32, (PW, PW), 1)
    eye = (row == col).astype(jnp.float32)
    power = [split(jnp.where(row > col, x, 0.0)) for x in squares[:2]]
    inverse = [eye - jnp.where(row > col, x, 0.0) for x in squares[:2]]
    for _ in range(1, PW.bit_length() - 1):
        power = [split(dot3(x, x)) for x in power]
        inverse = [x + dot3(split(x), y) for x, y in zip(inverse, power)]
    for p, x in enumerate(inverse + squares[2:]):
        high, low = split(x)
        high_ref[p] = high
        low_ref[p] = low


def squares_of(core, own, far):
    vmem = pl.BlockSpec(memory_space=pltpu.VMEM)
    pair = jax.ShapeDtypeStruct((4, PW, PW), jnp.bfloat16)
    return pl.pallas_call(
        squares_kernel,
        out_shape=(pair, pair),
        in_specs=[pl.BlockSpec(memory_space=pltpu.SMEM), vmem, vmem],
        out_specs=(vmem, vmem),
        cost_estimate=pl.CostEstimate(flops=6 * 28 * PW**3, bytes_accessed=2 << 20, transcendentals=0),
        compiler_params=pltpu.CompilerParams(vmem_limit_bytes=LIMIT),
        name="squares",
    )(core, own, far)


def lower_kernel(col_ref, near0_ref, near1_ref, near2_ref, near3_ref, high_ref, low_ref, turned_ref):
    x_at = col_ref[0] % NX
    for bits, ref in enumerate((near0_ref, near1_ref, near2_ref, near3_ref)):
        x = x_at ^ bits
        for i, y in enumerate(TURN):
            at = pl.multiple_of((NX * y + x) * 8, 8)
            for p in range(2):
                for h in range(4):
                    tile = ref[i, 32 * p + 8 * h : 32 * p + 8 * h + 8, :]
                    turned_ref[p, pl.ds(at, 8), 128 * h : 128 * h + 128] = tile

    for p in range(2):
        high, low = split(turned_ref[p].T)
        high_ref[p] = high
        low_ref[p] = low


def lower_of(col, *near):
    vmem = pl.BlockSpec(memory_space=pltpu.VMEM)
    pair = jax.ShapeDtypeStruct((2, 512, PW), jnp.bfloat16)
    return pl.pallas_call(
        lower_kernel,
        out_shape=(pair, pair),
        in_specs=[pl.BlockSpec(memory_space=pltpu.SMEM)] + [vmem] * 4,
        out_specs=(vmem, vmem),
        scratch_shapes=[pltpu.VMEM((2, PW, 512), jnp.float32)],
        cost_estimate=pl.CostEstimate(flops=1 << 20, bytes_accessed=2 << 20, transcendentals=0),
        compiler_params=pltpu.CompilerParams(vmem_limit_bytes=LIMIT),
        name="lower",
    )(col, *near)


def update_kernel(me_ref, piv_ref, wide_ref, sq_high_ref, sq_low_ref, lo_high_ref, lo_low_ref, block_ref, out_ref):
    me = me_ref[0]
    start = me * 512

    def rows(at):
        return wide_ref[:, at : at + 32, :].reshape(PW, 128)

    square = [(sq_high_ref[p], sq_low_ref[p]) for p in range(4)]
    upper0 = dot3_narrow(square[0], split(rows(0)))
    pair0 = split(upper0)
    upper1 = dot3_narrow(square[1], split(rows(64) - dot3_narrow(square[3], pair0)))

    @pl.when(me == 0)
    def _():
        out_ref[:PW] = upper0
        out_ref[PW:] = upper1

    @pl.when(me != 0)
    def _():
        second = rows(96) - dot3_narrow(square[2], pair0)
        at = lax.broadcasted_iota(jnp.int32, (512, PW), 0) + start

        def place(p, x, work):
            select = (at == piv_ref[p : p + 1, :]).astype(jnp.bfloat16)
            high = x.astype(jnp.bfloat16)
            rest = x - high.astype(jnp.float32)
            mid = rest.astype(jnp.bfloat16)
            low = (rest - mid.astype(jnp.float32)).astype(jnp.bfloat16)
            one = dot(select, jnp.concatenate([high, jnp.ones((PW, 128), jnp.bfloat16)], 1))
            two = dot(select, jnp.concatenate([mid, low], 1))
            moved = one[:, :128] + two[:, :128] + two[:, 128:]
            return jnp.where(one[:, 128:] > 0, moved, work)

        work = place(0, rows(32), block_ref[...])
        work = work - dot3_narrow((lo_high_ref[0], lo_low_ref[0]), pair0)
        work = place(1, second, work)
        out_ref[...] = work - dot3_narrow((lo_high_ref[1], lo_low_ref[1]), split(upper1))


def update_of(me, pivots, wide, squares, lower, block):
    vmem = pl.BlockSpec(memory_space=pltpu.VMEM)
    return pl.pallas_call(
        update_kernel,
        out_shape=jax.ShapeDtypeStruct((512, 128), jnp.float32),
        in_specs=[pl.BlockSpec(memory_space=pltpu.SMEM)] + [vmem] * 7,
        out_specs=vmem,
        cost_estimate=pl.CostEstimate(flops=1 << 29, bytes_accessed=3 << 20, transcendentals=0),
        compiler_params=pltpu.CompilerParams(vmem_limit_bytes=LIMIT),
        name="update",
    )(me, pivots, wide, *squares, *lower, block)


def step(block, panels, pivots):
    me = lax.axis_index("row")
    core = me % NC
    start = me * 512
    first = me == 0
    p0, p1 = pivots[0], pivots[1]
    j = jnp.arange(PW, dtype=jnp.int32)
    lane = jnp.arange(512, dtype=jnp.int32)

    def through0(rows):
        hit = p0[None, :] == rows[:, None]
        found = jnp.max(jnp.where(hit, j[None, :], -1), axis=1)
        return jnp.where(found >= 0, found, rows)

    source = jnp.concatenate([p0, through0(p1), j, through0(PW + j)])
    pick = (source[:, None] - start == lane[None, :]).astype(jnp.float32)
    rows = mm(pick, block).reshape(2, NC, NZ, 32, 128)
    rows = rows.transpose(1, 2, 0, 3, 4).reshape(NC, NZ, 64, 128)

    pan_t = panels.transpose(0, 2, 1)
    near = pan_t.reshape(2, 8, 4, 128).transpose(0, 2, 1, 3).reshape(64, 128)
    near = spread(near, "col", Y_GROUPS)

    at1 = (p1[:, None] - start == lane[None, :]).astype(jnp.float32)
    piv_t = mm(pan_t[0], at1, 1, 1)
    zero = jnp.zeros((8, PW), jnp.float32)
    own = lambda t: jnp.where(first, t, zero)
    pieces = jnp.stack([own(pan_t[0, :, :PW]), own(pan_t[1, :, PW:]), own(pan_t[0, :, PW:]), piv_t])
    tiles = pieces.reshape(4, 8, 2, 128).transpose(2, 0, 1, 3).reshape(2, 32, 128)

    def side(pair, mine):
        return jnp.where((core == 0) == mine, pair[0], pair[1])

    def halves(mine):
        return jnp.concatenate([side(rows, mine).reshape(512, 128), side(tiles, mine)], 0)

    part = halves(True) + lax.ppermute(halves(False), "row", PAIR)
    part = jnp.concatenate(
        [part[:512].reshape(NZ, 64, 128), jnp.broadcast_to(part[None, 512:], (NZ, 32, 128))], 1
    )
    part, near = lax.optimization_barrier((part, near))

    part = lax.all_to_all(part, "row", 0, 0, tiled=True, axis_index_groups=Z_GROUPS)
    near1 = flip(near, 1)
    part, near, near1 = lax.optimization_barrier((part, near, near1))

    part = jnp.sum(part, 0)
    tile = jnp.broadcast_to(part[64:], (NX * NY, 32, 128))
    tile = lax.all_to_all(tile, "col", 0, 0, tiled=True, axis_index_groups=COL_GROUPS)
    near2 = flip(near, 2)
    far = lax.ppermute(part[:64], "row", PAIR)
    both = jnp.where(core == 0, jnp.concatenate([part[:64], far]), jnp.concatenate([far, part[:64]]))
    tile, both, near2 = lax.optimization_barrier((tile, both, near2))

    wide = spread(both, "row", Z_GROUPS)
    far = lax.ppermute(tile, "row", PAIR)
    near3 = flip(near, 3)
    squares = squares_of(core.reshape(1), tile, far)
    lower = lower_of(lax.axis_index("col").reshape(1), near, near1, near2, near3)
    wide, squares, lower = lax.optimization_barrier((wide, squares, lower))
    return update_of(me.reshape(1), pivots, wide, squares, lower, block)


def solution(mesh):
    return jax.shard_map(
        step,
        mesh=mesh,
        in_specs=(P("row", "col"), P(None, "row", "col"), P()),
        out_specs=P("row", "col"),
        check_vma=False,
    )
```

```python
import jax
import jax.numpy as jnp
from jax import lax
from jax.experimental import pallas as pl
from jax.experimental.pallas import tpu as pltpu
from jax.sharding import PartitionSpec as P


PW = 256
LIMIT = 16 << 20
NZ, NC = 8, 2
NY, NX = 8, 4
TURN = [0, 4, 2, 6, 3, 7, 1, 5]
Z_GROUPS = [[NC * z + core for z in TURN] for core in range(NC)]
Y_GROUPS = [[NX * y + x for y in TURN] for x in range(NX)]
COL_GROUPS = [[NX * y + x for x in (0, 2, 1, 3) for y in range(NY)]]
PAIR = [(i, i ^ 1) for i in range(NZ * NC)]


def mm(a, b, ca=1, cb=0):
    return lax.dot_general(
        a, b, (((ca,), (cb,)), ((), ())),
        precision=lax.Precision.HIGH, preferred_element_type=jnp.float32,
    )


def spread(x, axis, groups):
    n = len(groups[0])
    return lax.all_to_all(
        jnp.broadcast_to(x[None], (n,) + x.shape), axis, 0, 0, tiled=True, axis_index_groups=groups
    )


def flip(x, bits):
    return lax.ppermute(x, "col", [(i, i ^ bits) for i in range(NX * NY)])


def split(x):
    high = x.astype(jnp.bfloat16)
    return high, (x - high.astype(jnp.float32)).astype(jnp.bfloat16)


def dot(a, b):
    return jnp.dot(a, b, preferred_element_type=jnp.float32)


def dot3(a, b):
    return dot(a[0], b[0]) + dot(a[0], b[1]) + dot(a[1], b[0])


def dot3_narrow(a, b):
    both = dot(a[0], jnp.concatenate(b, 1))
    return both[:, :128] + both[:, 128:] + dot(a[1], b[0])


def halves_of(core, own, far):
    return jnp.where(core == 0, own, far), jnp.where(core == 0, far, own)


def squares_kernel(core_ref, own_ref, far_ref, high_ref, low_ref):
    core = core_ref[0]
    squares = []
    for p in range(4):
        order = [COL_GROUPS[0].index(c) for c in range(NX * NY)]
        own = jnp.concatenate([own_ref[i, 8 * p : 8 * p + 8, :] for i in order], 0)
        far = jnp.concatenate([far_ref[i, 8 * p : 8 * p + 8, :] for i in order], 0)
        squares.append(jnp.concatenate(halves_of(core, own, far), 1).T)
    row = lax.broadcasted_iota(jnp.int32, (PW, PW), 0)
    col = lax.broadcasted_iota(jnp.int32, (PW, PW), 1)
    eye = (row == col).astype(jnp.float32)
    power = [split(jnp.where(row > col, x, 0.0)) for x in squares[:2]]
    inverse = [eye - jnp.where(row > col, x, 0.0) for x in squares[:2]]
    for _ in range(1, PW.bit_length() - 1):
        power = [split(dot3(x, x)) for x in power]
        inverse = [x + dot3(split(x), y) for x, y in zip(inverse, power)]
    for p, x in enumerate(inverse + squares[2:]):
        high, low = split(x)
        high_ref[p] = high
        low_ref[p] = low


def squares_of(core, own, far):
    vmem = pl.BlockSpec(memory_space=pltpu.VMEM)
    pair = jax.ShapeDtypeStruct((4, PW, PW), jnp.bfloat16)
    return pl.pallas_call(
        squares_kernel,
        out_shape=(pair, pair),
        in_specs=[pl.BlockSpec(memory_space=pltpu.SMEM), vmem, vmem],
        out_specs=(vmem, vmem),
        cost_estimate=pl.CostEstimate(flops=6 * 28 * PW**3, bytes_accessed=2 << 20, transcendentals=0),
        compiler_params=pltpu.CompilerParams(vmem_limit_bytes=LIMIT),
        name="squares",
    )(core, own, far)


def update_kernel(
    at_ref, piv_ref, wide_ref, sq_high_ref, sq_low_ref, block_ref, n0_ref, n1_ref, n2_ref, n3_ref,
    out_ref, near_ref, turned_ref, sems,
):
    me = at_ref[0]
    copies = [
        pltpu.make_async_copy(ref, near_ref.at[bits], sems.at[bits])
        for bits, ref in enumerate((n0_ref, n1_ref, n2_ref, n3_ref))
    ]
    for copy in copies:
        copy.start()
    start = me * 512

    def rows(at):
        return wide_ref[:, at : at + 32, :].reshape(PW, 128)

    square = [(sq_high_ref[p], sq_low_ref[p]) for p in range(4)]
    upper0 = dot3_narrow(square[0], split(rows(0)))
    pair0 = split(upper0)
    upper1 = dot3_narrow(square[1], split(rows(64) - dot3_narrow(square[3], pair0)))

    for bits, copy in enumerate(copies):
        copy.wait()
        x = (at_ref[1] % NX) ^ bits
        for i, y in enumerate(TURN):
            at = pl.multiple_of((NX * y + x) * 8, 8)
            for p in range(2):
                for h in range(4):
                    tile = near_ref[bits, i, 32 * p + 8 * h : 32 * p + 8 * h + 8, :]
                    turned_ref[p, pl.ds(at, 8), 128 * h : 128 * h + 128] = tile

    @pl.when(me == 0)
    def _():
        out_ref[:PW] = upper0
        out_ref[PW:] = upper1

    @pl.when(me != 0)
    def _():
        second = rows(96) - dot3_narrow(square[2], pair0)
        at = lax.broadcasted_iota(jnp.int32, (512, PW), 0) + start

        def place(p, x, work):
            select = (at == piv_ref[p : p + 1, :]).astype(jnp.bfloat16)
            high = x.astype(jnp.bfloat16)
            rest = x - high.astype(jnp.float32)
            mid = rest.astype(jnp.bfloat16)
            low = (rest - mid.astype(jnp.float32)).astype(jnp.bfloat16)
            one = dot(select, jnp.concatenate([high, jnp.ones((PW, 128), jnp.bfloat16)], 1))
            two = dot(select, jnp.concatenate([mid, low], 1))
            moved = one[:, :128] + two[:, :128] + two[:, 128:]
            return jnp.where(one[:, 128:] > 0, moved, work)

        work = place(0, rows(32), block_ref[...])
        work = work - dot3_narrow(split(turned_ref[0].T), pair0)
        work = place(1, second, work)
        out_ref[...] = work - dot3_narrow(split(turned_ref[1].T), split(upper1))


def update_of(at, pivots, wide, squares, block, near):
    vmem = pl.BlockSpec(memory_space=pltpu.VMEM)
    return pl.pallas_call(
        update_kernel,
        out_shape=jax.ShapeDtypeStruct((512, 128), jnp.float32),
        in_specs=[pl.BlockSpec(memory_space=pltpu.SMEM)] + [vmem] * 5 + [pl.BlockSpec(memory_space=pl.ANY)] * 4,
        out_specs=vmem,
        scratch_shapes=[
            pltpu.VMEM((NX, NY, 64, 128), jnp.float32),
            pltpu.VMEM((2, PW, 512), jnp.float32),
            pltpu.SemaphoreType.DMA((NX,)),
        ],
        cost_estimate=pl.CostEstimate(flops=1 << 29, bytes_accessed=3 << 20, transcendentals=0),
        compiler_params=pltpu.CompilerParams(vmem_limit_bytes=LIMIT),
        name="update",
    )(at, pivots, wide, *squares, block, *near)


def step(block, panels, pivots):
    me = lax.axis_index("row")
    core = me % NC
    start = me * 512
    first = me == 0
    p0, p1 = pivots[0], pivots[1]
    j = jnp.arange(PW, dtype=jnp.int32)
    lane = jnp.arange(512, dtype=jnp.int32)

    def through0(rows):
        hit = p0[None, :] == rows[:, None]
        found = jnp.max(jnp.where(hit, j[None, :], -1), axis=1)
        return jnp.where(found >= 0, found, rows)

    source = jnp.concatenate([p0, through0(p1), j, through0(PW + j)])
    pick = (source[:, None] - start == lane[None, :]).astype(jnp.float32)
    rows = mm(pick, block).reshape(2, NC, NZ, 32, 128)
    rows = rows.transpose(1, 2, 0, 3, 4).reshape(NC, NZ, 64, 128)

    pan_t = panels.transpose(0, 2, 1)
    near = pan_t.reshape(2, 8, 4, 128).transpose(0, 2, 1, 3).reshape(64, 128)
    near = spread(near, "col", Y_GROUPS)

    at1 = (p1[:, None] - start == lane[None, :]).astype(jnp.float32)
    piv_t = mm(pan_t[0], at1, 1, 1)
    zero = jnp.zeros((8, PW), jnp.float32)
    own = lambda t: jnp.where(first, t, zero)
    pieces = jnp.stack([own(pan_t[0, :, :PW]), own(pan_t[1, :, PW:]), own(pan_t[0, :, PW:]), piv_t])
    tiles = pieces.reshape(4, 8, 2, 128).transpose(2, 0, 1, 3).reshape(2, 32, 128)

    def side(pair, mine):
        return jnp.where((core == 0) == mine, pair[0], pair[1])

    def halves(mine):
        return jnp.concatenate([side(rows, mine).reshape(512, 128), side(tiles, mine)], 0)

    part = halves(True) + lax.ppermute(halves(False), "row", PAIR)
    part = jnp.concatenate(
        [part[:512].reshape(NZ, 64, 128), jnp.broadcast_to(part[None, 512:], (NZ, 32, 128))], 1
    )
    part, near = lax.optimization_barrier((part, near))

    part = lax.all_to_all(part, "row", 0, 0, tiled=True, axis_index_groups=Z_GROUPS)
    near1 = flip(near, 1)
    part, near, near1 = lax.optimization_barrier((part, near, near1))

    part = jnp.sum(part, 0)
    tile = jnp.broadcast_to(part[64:], (NX * NY, 32, 128))
    tile = lax.all_to_all(tile, "col", 0, 0, tiled=True, axis_index_groups=COL_GROUPS)
    near2 = flip(near, 2)
    far = lax.ppermute(part[:64], "row", PAIR)
    both = jnp.where(core == 0, jnp.concatenate([part[:64], far]), jnp.concatenate([far, part[:64]]))
    tile, both, near2 = lax.optimization_barrier((tile, both, near2))

    wide = spread(both, "row", Z_GROUPS)
    far = lax.ppermute(tile, "row", PAIR)
    near3 = flip(near, 3)
    squares = squares_of(core.reshape(1), tile, far)
    wide, squares = lax.optimization_barrier((wide, squares))
    at = jnp.stack([me, lax.axis_index("col")])
    return update_of(at, pivots, wide, squares, block, (near, near1, near2, near3))


def solution(mesh):
    return jax.shard_map(
        step,
        mesh=mesh,
        in_specs=(P("row", "col"), P(None, "row", "col"), P()),
        out_specs=P("row", "col"),
        check_vma=False,
    )
```

```python
import jax
import jax.numpy as jnp
from jax import lax
from jax.experimental import pallas as pl
from jax.experimental.pallas import tpu as pltpu
from jax.sharding import PartitionSpec as P


PW = 256
LIMIT = 16 << 20
NZ, NC = 8, 2
NY, NX = 8, 4
TURN = [0, 4, 2, 6, 3, 7, 1, 5]
Z_GROUPS = [[NC * z + core for z in TURN] for core in range(NC)]
Y_GROUPS = [[NX * y + x for y in TURN] for x in range(NX)]
COL_GROUPS = [[NX * y + x for x in (0, 2, 1, 3) for y in range(NY)]]
PAIR = [(i, i ^ 1) for i in range(NZ * NC)]


def mm(a, b, ca=1, cb=0):
    return lax.dot_general(
        a, b, (((ca,), (cb,)), ((), ())),
        precision=lax.Precision.HIGH, preferred_element_type=jnp.float32,
    )


def spread(x, axis, groups):
    n = len(groups[0])
    return lax.all_to_all(
        jnp.broadcast_to(x[None], (n,) + x.shape), axis, 0, 0, tiled=True, axis_index_groups=groups
    )


def flip(x, bits):
    return lax.ppermute(x, "col", [(i, i ^ bits) for i in range(NX * NY)])


def split(x):
    high = x.astype(jnp.bfloat16)
    return high, (x - high.astype(jnp.float32)).astype(jnp.bfloat16)


def dot(a, b):
    return jnp.dot(a, b, preferred_element_type=jnp.float32)


def dot3(a, b):
    return dot(a[0], b[0]) + dot(a[0], b[1]) + dot(a[1], b[0])


def dot3_narrow(a, b):
    both = dot(a[0], jnp.concatenate(b, 1))
    return both[:, :128] + both[:, 128:] + dot(a[1], b[0])


def halves_of(core, own, far):
    return jnp.where(core == 0, own, far), jnp.where(core == 0, far, own)


def squares_kernel(core_ref, own_ref, far_ref, high_ref, low_ref):
    core = core_ref[0]
    squares = []
    for p in range(4):
        order = [COL_GROUPS[0].index(c) for c in range(NX * NY)]
        own = jnp.concatenate([own_ref[i, 8 * p : 8 * p + 8, :] for i in order], 0)
        far = jnp.concatenate([far_ref[i, 8 * p : 8 * p + 8, :] for i in order], 0)
        squares.append(jnp.concatenate(halves_of(core, own, far), 1).T)
    row = lax.broadcasted_iota(jnp.int32, (PW, PW), 0)
    col = lax.broadcasted_iota(jnp.int32, (PW, PW), 1)
    eye = (row == col).astype(jnp.float32)
    power = [split(jnp.where(row > col, x, 0.0)) for x in squares[:2]]
    inverse = [eye - jnp.where(row > col, x, 0.0) for x in squares[:2]]
    for _ in range(1, PW.bit_length() - 1):
        power = [split(dot3(x, x)) for x in power]
        inverse = [x + dot3(split(x), y) for x, y in zip(inverse, power)]
    for p, x in enumerate(inverse + squares[2:]):
        high, low = split(x)
        high_ref[p] = high
        low_ref[p] = low


def squares_of(core, own, far):
    vmem = pl.BlockSpec(memory_space=pltpu.VMEM)
    pair = jax.ShapeDtypeStruct((4, PW, PW), jnp.bfloat16)
    return pl.pallas_call(
        squares_kernel,
        out_shape=(pair, pair),
        in_specs=[pl.BlockSpec(memory_space=pltpu.SMEM), vmem, vmem],
        out_specs=(vmem, vmem),
        cost_estimate=pl.CostEstimate(flops=6 * 28 * PW**3, bytes_accessed=2 << 20, transcendentals=0),
        compiler_params=pltpu.CompilerParams(vmem_limit_bytes=LIMIT),
        name="squares",
    )(core, own, far)


def update_kernel(
    at_ref, piv_ref, col_ref, local_ref, wide_ref, sq_high_ref, sq_low_ref, block_ref, n0_ref, n1_ref, n2_ref, n3_ref,
    out_ref, near_ref, turned_ref, sems,
):
    me = at_ref[0]
    copies = [
        pltpu.make_async_copy(ref, near_ref.at[bits], sems.at[bits])
        for bits, ref in enumerate((n0_ref, n1_ref, n2_ref, n3_ref))
    ]
    for copy in copies:
        copy.start()
    start = me * 512

    got = [wide_ref[:, 32 * p : 32 * p + 32, :].reshape(PW, 128) for p in range(2)]
    held = [local_ref[:PW], local_ref[PW:]]
    named = [jnp.broadcast_to(col_ref[:, p : p + 1], (PW, PW)) for p in range(2)]
    again = jnp.logical_and(named[1] == piv_ref[0:1, :], me != 0).astype(jnp.bfloat16)
    twice = dot(again, jnp.concatenate(split(got[0]), 1))
    held[1] = held[1] + twice[:, :128] + twice[:, 128:]
    top = [jnp.where(lax.shift_right_logical(named[p][:, :128], 9) == me, held[p], got[p]) for p in range(2)]

    square = [(sq_high_ref[p], sq_low_ref[p]) for p in range(4)]
    upper0 = dot3_narrow(square[0], split(top[0]))
    pair0 = split(upper0)
    upper1 = dot3_narrow(square[1], split(top[1] - dot3_narrow(square[3], pair0)))

    for bits, copy in enumerate(copies):
        copy.wait()
        x = (at_ref[1] % NX) ^ bits
        for i, y in enumerate(TURN):
            at = pl.multiple_of((NX * y + x) * 8, 8)
            for p in range(2):
                for h in range(4):
                    tile = near_ref[bits, i, 32 * p + 8 * h : 32 * p + 8 * h + 8, :]
                    turned_ref[p, pl.ds(at, 8), 128 * h : 128 * h + 128] = tile

    @pl.when(me == 0)
    def _():
        out_ref[:PW] = upper0
        out_ref[PW:] = upper1

    @pl.when(me != 0)
    def _():
        second = got[1] - dot3_narrow(square[2], pair0)
        at = lax.broadcasted_iota(jnp.int32, (512, PW), 0) + start

        def place(p, x, work):
            select = (at == piv_ref[p : p + 1, :]).astype(jnp.bfloat16)
            high = x.astype(jnp.bfloat16)
            rest = x - high.astype(jnp.float32)
            mid = rest.astype(jnp.bfloat16)
            low = (rest - mid.astype(jnp.float32)).astype(jnp.bfloat16)
            one = dot(select, jnp.concatenate([high, jnp.ones((PW, 128), jnp.bfloat16)], 1))
            two = dot(select, jnp.concatenate([mid, low], 1))
            moved = one[:, :128] + two[:, :128] + two[:, 128:]
            return jnp.where(one[:, 128:] > 0, moved, work)

        work = place(0, got[0], block_ref[...])
        work = work - dot3_narrow(split(turned_ref[0].T), pair0)
        work = place(1, second, work)
        out_ref[...] = work - dot3_narrow(split(turned_ref[1].T), split(upper1))


def update_of(at, pivots, local, wide, squares, block, near):
    vmem = pl.BlockSpec(memory_space=pltpu.VMEM)
    return pl.pallas_call(
        update_kernel,
        out_shape=jax.ShapeDtypeStruct((512, 128), jnp.float32),
        in_specs=[pl.BlockSpec(memory_space=pltpu.SMEM)] + [vmem] * 7 + [pl.BlockSpec(memory_space=pl.ANY)] * 4,
        out_specs=vmem,
        scratch_shapes=[
            pltpu.VMEM((NX, NY, 64, 128), jnp.float32),
            pltpu.VMEM((2, PW, 512), jnp.float32),
            pltpu.SemaphoreType.DMA((NX,)),
        ],
        cost_estimate=pl.CostEstimate(flops=1 << 29, bytes_accessed=3 << 20, transcendentals=0),
        compiler_params=pltpu.CompilerParams(vmem_limit_bytes=LIMIT),
        name="update",
    )(at, pivots, pivots.T, local, wide, *squares, block, *near)


def step(block, panels, pivots):
    me = lax.axis_index("row")
    core = me % NC
    start = me * 512
    first = me == 0
    p0, p1 = pivots[0], pivots[1]
    j = jnp.arange(PW, dtype=jnp.int32)
    lane = jnp.arange(512, dtype=jnp.int32)

    def through0(rows):
        hit = p0[None, :] == rows[:, None]
        found = jnp.max(jnp.where(hit, j[None, :], -1), axis=1)
        return jnp.where(found >= 0, found, rows)

    source = jnp.concatenate([p0, through0(p1), j, through0(PW + j)])
    pick = (source[:, None] - start == lane[None, :]).astype(jnp.float32)
    picked = mm(pick, block)
    rows = picked.reshape(2, NC, NZ, 32, 128)
    rows = rows.transpose(1, 2, 0, 3, 4).reshape(NC, NZ, 64, 128)

    pan_t = panels.transpose(0, 2, 1)
    near = pan_t.reshape(2, 8, 4, 128).transpose(0, 2, 1, 3).reshape(64, 128)
    near = spread(near, "col", Y_GROUPS)

    at1 = (p1[:, None] - start == lane[None, :]).astype(jnp.float32)
    piv_t = mm(pan_t[0], at1, 1, 1)
    zero = jnp.zeros((8, PW), jnp.float32)
    own = lambda t: jnp.where(first, t, zero)
    pieces = jnp.stack([own(pan_t[0, :, :PW]), own(pan_t[1, :, PW:]), own(pan_t[0, :, PW:]), piv_t])
    tiles = pieces.reshape(4, 8, 2, 128).transpose(2, 0, 1, 3).reshape(2, 32, 128)

    def side(pair, mine):
        return jnp.where((core == 0) == mine, pair[0], pair[1])

    def halves(mine):
        return jnp.concatenate([side(rows, mine).reshape(512, 128), side(tiles, mine)], 0)

    part = halves(True) + lax.ppermute(halves(False), "row", PAIR)
    part = jnp.concatenate(
        [part[:512].reshape(NZ, 64, 128), jnp.broadcast_to(part[None, 512:], (NZ, 32, 128))], 1
    )
    part, near = lax.optimization_barrier((part, near))

    part = lax.all_to_all(part, "row", 0, 0, tiled=True, axis_index_groups=Z_GROUPS)
    near1 = flip(near, 1)
    part, near, near1 = lax.optimization_barrier((part, near, near1))

    part = jnp.sum(part, 0)
    tile = jnp.broadcast_to(part[64:], (NX * NY, 32, 128))
    tile = lax.all_to_all(tile, "col", 0, 0, tiled=True, axis_index_groups=COL_GROUPS)
    near2 = flip(near, 2)
    far = lax.ppermute(part[:64], "row", PAIR)
    mine = part[:64].reshape(2, 32, 128)
    far = far.reshape(2, 32, 128)
    both = jnp.where(core == 0, jnp.stack([mine, far]), jnp.stack([far, mine]))
    turn = jnp.array(TURN, jnp.int32)
    here = (turn == me // NC)[None, :, None]
    place = jnp.sum(jnp.where(here, pivots.reshape(2, NZ, 32), 0), 1) // 512
    owner = (NC * turn + core)[:, None, None] == place[None]
    wide = jnp.where(owner[..., None], both[None, :, 1], both[None, :, 0]).reshape(NZ, 64, 128)
    tile, wide, near2 = lax.optimization_barrier((tile, wide, near2))

    wide = lax.all_to_all(wide, "row", 0, 0, tiled=True, axis_index_groups=Z_GROUPS)
    far = lax.ppermute(tile, "row", PAIR)
    near3 = flip(near, 3)
    squares = squares_of(core.reshape(1), tile, far)
    wide, squares = lax.optimization_barrier((wide, squares))
    at = jnp.stack([me, lax.axis_index("col")])
    near, near1, near2, near3 = (pltpu.with_memory_space_constraint(x, pltpu.HBM) for x in (near, near1, near2, near3))
    return update_of(at, pivots, picked[:512], wide, squares, block, (near, near1, near2, near3))


def solution(mesh):
    return jax.shard_map(
        step,
        mesh=mesh,
        in_specs=(P("row", "col"), P(None, "row", "col"), P()),
        out_specs=P("row", "col"),
        check_vma=False,
    )
```

```python
import jax
import jax.numpy as jnp
from jax import lax
from jax.experimental import pallas as pl
from jax.experimental.pallas import tpu as pltpu
from jax.sharding import PartitionSpec as P


PW = 256
LIMIT = 16 << 20
NZ, NC = 8, 2
NY, NX = 8, 4
TURN = [0, 4, 2, 6, 3, 7, 1, 5]
Z_GROUPS = [[NC * z + core for z in TURN] for core in range(NC)]
Y_GROUPS = [[NX * y + x for y in TURN] for x in range(NX)]
COL_GROUPS = [[NX * y + x for x in (0, 2, 1, 3) for y in range(NY)]]
PAIR = [(i, i ^ 1) for i in range(NZ * NC)]


def mm(a, b, ca=1, cb=0):
    return lax.dot_general(
        a, b, (((ca,), (cb,)), ((), ())),
        precision=lax.Precision.HIGH, preferred_element_type=jnp.float32,
    )


def spread(x, axis, groups):
    n = len(groups[0])
    return lax.all_to_all(
        jnp.broadcast_to(x[None], (n,) + x.shape), axis, 0, 0, tiled=True, axis_index_groups=groups
    )


def flip(x, bits):
    return lax.ppermute(x, "col", [(i, i ^ bits) for i in range(NX * NY)])


def split(x):
    high = x.astype(jnp.bfloat16)
    return high, (x - high.astype(jnp.float32)).astype(jnp.bfloat16)


def dot(a, b):
    return jnp.dot(a, b, preferred_element_type=jnp.float32)


def dot3(a, b):
    return dot(a[0], b[0]) + dot(a[0], b[1]) + dot(a[1], b[0])


def dot3_narrow(a, b):
    both = dot(a[0], jnp.concatenate(b, 1))
    return both[:, :128] + both[:, 128:] + dot(a[1], b[0])


def halves_of(core, own, far):
    return jnp.where(core == 0, own, far), jnp.where(core == 0, far, own)


def squares_kernel(core_ref, own_ref, far_ref, high_ref, low_ref):
    core = core_ref[0]
    squares = []
    for p in range(4):
        order = [COL_GROUPS[0].index(c) for c in range(NX * NY)]
        own = jnp.concatenate([own_ref[i, 8 * p : 8 * p + 8, :] for i in order], 0)
        far = jnp.concatenate([far_ref[i, 8 * p : 8 * p + 8, :] for i in order], 0)
        squares.append(jnp.concatenate(halves_of(core, own, far), 1).T)
    row = lax.broadcasted_iota(jnp.int32, (PW, PW), 0)
    col = lax.broadcasted_iota(jnp.int32, (PW, PW), 1)
    eye = (row == col).astype(jnp.float32)
    power = [split(jnp.where(row > col, x, 0.0)) for x in squares[:2]]
    inverse = [eye - jnp.where(row > col, x, 0.0) for x in squares[:2]]
    for level in range(1, PW.bit_length() - 1):
        cut = 1 << level if level >= 4 else 0

        def square(x):
            full = dot3((x[0][cut:], x[1][cut:]), x)
            return split(jnp.concatenate([jnp.zeros((cut, PW), jnp.float32), full], 0) if cut else full)

        def extend(x, y):
            full = x[cut:] + dot3(split(x[cut:]), y)
            return jnp.concatenate([x[:cut], full], 0) if cut else full

        power = [square(x) for x in power]
        inverse = [extend(x, y) for x, y in zip(inverse, power)]
    for p, x in enumerate(inverse + squares[2:]):
        high, low = split(x)
        high_ref[p] = high
        low_ref[p] = low


def squares_of(core, own, far):
    vmem = pl.BlockSpec(memory_space=pltpu.VMEM)
    pair = jax.ShapeDtypeStruct((4, PW, PW), jnp.bfloat16)
    return pl.pallas_call(
        squares_kernel,
        out_shape=(pair, pair),
        in_specs=[pl.BlockSpec(memory_space=pltpu.SMEM), vmem, vmem],
        out_specs=(vmem, vmem),
        cost_estimate=pl.CostEstimate(flops=6 * 28 * PW**3, bytes_accessed=2 << 20, transcendentals=0),
        compiler_params=pltpu.CompilerParams(vmem_limit_bytes=LIMIT),
        name="squares",
    )(core, own, far)


def update_kernel(
    at_ref, piv_ref, col_ref, local_ref, wide_ref, sq_high_ref, sq_low_ref, block_ref, n0_ref, n1_ref, n2_ref, n3_ref,
    out_ref, near_ref, turned_ref, sems,
):
    me = at_ref[0]
    copies = [
        pltpu.make_async_copy(ref, near_ref.at[bits], sems.at[bits])
        for bits, ref in enumerate((n0_ref, n1_ref, n2_ref, n3_ref))
    ]
    for copy in copies:
        copy.start()

    got = [wide_ref[:, 32 * p : 32 * p + 32, :].reshape(PW, 128) for p in range(2)]
    held = [local_ref[:PW], local_ref[PW:]]
    named = [jnp.broadcast_to(col_ref[:, p : p + 1], (PW, PW)) for p in range(2)]
    again = jnp.logical_and(named[1] == piv_ref[0:1, :], me != 0).astype(jnp.bfloat16)
    twice = dot(again, jnp.concatenate(split(got[0]), 1))
    held[1] = held[1] + twice[:, :128] + twice[:, 128:]
    top = [jnp.where(lax.shift_right_logical(named[p][:, :128], 9) == me, held[p], got[p]) for p in range(2)]

    for copy in copies:
        copy.wait()
    for bits in range(NX):
        x = (at_ref[1] % NX) ^ bits
        for i, y in enumerate(TURN):
            at = pl.multiple_of((NX * y + x) * 8, 8)
            for p in range(2):
                for h in range(4):
                    tile = near_ref[bits, i, 32 * p + 8 * h : 32 * p + 8 * h + 8, :]
                    turned_ref[p, pl.ds(at, 8), 128 * h : 128 * h + 128] = tile
    lower = [split(turned_ref[p].T) for p in range(2)]

    square = [(sq_high_ref[p], sq_low_ref[p]) for p in range(4)]
    upper0 = dot3_narrow(square[0], split(top[0]))
    pair0 = split(upper0)
    upper1 = dot3_narrow(square[1], split(top[1] - dot3_narrow(square[3], pair0)))
    second = got[1] - dot3_narrow(square[2], pair0)
    rank = lax.broadcasted_iota(jnp.int32, (512, PW), 0) + me * 512

    def place(p, x, work):
        select = (rank == piv_ref[p : p + 1, :]).astype(jnp.bfloat16)
        high = x.astype(jnp.bfloat16)
        rest = x - high.astype(jnp.float32)
        mid = rest.astype(jnp.bfloat16)
        low = (rest - mid.astype(jnp.float32)).astype(jnp.bfloat16)
        one = dot(select, jnp.concatenate([high, jnp.ones((PW, 128), jnp.bfloat16)], 1))
        two = dot(select, jnp.concatenate([mid, low], 1))
        moved = one[:, :128] + two[:, :128] + two[:, 128:]
        return jnp.where(one[:, 128:] > 0, moved, work)

    work = place(0, got[0], block_ref[...])
    work = work - dot3_narrow(lower[0], pair0)
    work = place(1, second, work)
    work = work - dot3_narrow(lower[1], split(upper1))
    out_ref[:PW] = jnp.where(me == 0, upper0, work[:PW])
    out_ref[PW:] = jnp.where(me == 0, upper1, work[PW:])


def update_of(at, pivots, local, wide, squares, block, near):
    vmem = pl.BlockSpec(memory_space=pltpu.VMEM)
    return pl.pallas_call(
        update_kernel,
        out_shape=jax.ShapeDtypeStruct((512, 128), jnp.float32),
        in_specs=[pl.BlockSpec(memory_space=pltpu.SMEM)] + [vmem] * 7 + [pl.BlockSpec(memory_space=pl.ANY)] * 4,
        out_specs=vmem,
        scratch_shapes=[
            pltpu.VMEM((NX, NY, 64, 128), jnp.float32),
            pltpu.VMEM((2, PW, 512), jnp.float32),
            pltpu.SemaphoreType.DMA((NX,)),
        ],
        cost_estimate=pl.CostEstimate(flops=1 << 29, bytes_accessed=3 << 20, transcendentals=0),
        compiler_params=pltpu.CompilerParams(vmem_limit_bytes=LIMIT),
        name="update",
    )(at, pivots, pivots.T, local, wide, *squares, block, *near)


def step(block, panels, pivots):
    me = lax.axis_index("row")
    core = me % NC
    start = me * 512
    first = me == 0
    p0, p1 = pivots[0], pivots[1]
    j = jnp.arange(PW, dtype=jnp.int32)
    lane = jnp.arange(512, dtype=jnp.int32)

    def through0(rows):
        hit = p0[None, :] == rows[:, None]
        found = jnp.max(jnp.where(hit, j[None, :], -1), axis=1)
        return jnp.where(found >= 0, found, rows)

    source = jnp.concatenate([p0, through0(p1), j, through0(PW + j)])
    pick = (source[:, None] - start == lane[None, :]).astype(jnp.float32)
    picked = mm(pick, block)
    rows = picked.reshape(2, NC, NZ, 32, 128)
    rows = rows.transpose(1, 2, 0, 3, 4).reshape(NC, NZ, 64, 128)

    pan_t = panels.transpose(0, 2, 1)
    near = pan_t.reshape(2, 8, 4, 128).transpose(0, 2, 1, 3).reshape(64, 128)
    near = spread(near, "col", Y_GROUPS)

    at1 = (p1[:, None] - start == lane[None, :]).astype(jnp.float32)
    piv_t = mm(pan_t[0], at1, 1, 1)
    zero = jnp.zeros((8, PW), jnp.float32)
    own = lambda t: jnp.where(first, t, zero)
    pieces = jnp.stack([own(pan_t[0, :, :PW]), own(pan_t[1, :, PW:]), own(pan_t[0, :, PW:]), piv_t])
    tiles = pieces.reshape(4, 8, 2, 128).transpose(2, 0, 1, 3).reshape(2, 32, 128)

    def side(pair, mine):
        return jnp.where((core == 0) == mine, pair[0], pair[1])

    def halves(mine):
        return jnp.concatenate([side(rows, mine).reshape(512, 128), side(tiles, mine)], 0)

    part = halves(True) + lax.ppermute(halves(False), "row", PAIR)
    part = jnp.concatenate(
        [part[:512].reshape(NZ, 64, 128), jnp.broadcast_to(part[None, 512:], (NZ, 32, 128))], 1
    )
    part, near = lax.optimization_barrier((part, near))

    part = lax.all_to_all(part, "row", 0, 0, tiled=True, axis_index_groups=Z_GROUPS)
    near1 = flip(near, 1)
    part, near, near1 = lax.optimization_barrier((part, near, near1))

    part = jnp.sum(part, 0)
    tile = jnp.broadcast_to(part[64:], (NX * NY, 32, 128))
    tile = lax.all_to_all(tile, "col", 0, 0, tiled=True, axis_index_groups=COL_GROUPS)
    near2 = flip(near, 2)
    far = lax.ppermute(part[:64], "row", PAIR)
    mine = part[:64].reshape(2, 32, 128)
    far = far.reshape(2, 32, 128)
    both = jnp.where(core == 0, jnp.stack([mine, far]), jnp.stack([far, mine]))
    turn = jnp.array(TURN, jnp.int32)
    here = (turn == me // NC)[None, :, None]
    place = jnp.sum(jnp.where(here, pivots.reshape(2, NZ, 32), 0), 1) // 512
    owner = (NC * turn + core)[:, None, None] == place[None]
    wide = jnp.where(owner[..., None], both[None, :, 1], both[None, :, 0]).reshape(NZ, 64, 128)
    tile, wide, near2 = lax.optimization_barrier((tile, wide, near2))

    wide = lax.all_to_all(wide, "row", 0, 0, tiled=True, axis_index_groups=Z_GROUPS)
    far = lax.ppermute(tile, "row", PAIR)
    near3 = flip(near, 3)
    squares = squares_of(core.reshape(1), tile, far)
    wide, squares = lax.optimization_barrier((wide, squares))
    at = jnp.stack([me, lax.axis_index("col")])
    near, near1, near2, near3 = (pltpu.with_memory_space_constraint(x, pltpu.HBM) for x in (near, near1, near2, near3))
    return update_of(at, pivots, picked[:512], wide, squares, block, (near, near1, near2, near3))


def solution(mesh):
    return jax.shard_map(
        step,
        mesh=mesh,
        in_specs=(P("row", "col"), P(None, "row", "col"), P()),
        out_specs=P("row", "col"),
        check_vma=False,
    )
```

```python
import jax
import jax.numpy as jnp
from jax import lax
from jax.experimental import pallas as pl
from jax.experimental.pallas import tpu as pltpu
from jax.sharding import PartitionSpec as P


PW = 256
LIMIT = 16 << 20
NZ, NC = 8, 2
NY, NX = 8, 4
TURN = [0, 4, 2, 6, 3, 7, 1, 5]
Z_GROUPS = [[NC * z + core for z in TURN] for core in range(NC)]
Y_GROUPS = [[NX * y + x for y in TURN] for x in range(NX)]
COL_GROUPS = [[NX * y + x for x in (0, 2, 1, 3) for y in range(NY)]]
PAIR = [(i, i ^ 1) for i in range(NZ * NC)]


def mm(a, b, ca=1, cb=0):
    return lax.dot_general(
        a, b, (((ca,), (cb,)), ((), ())),
        precision=lax.Precision.HIGH, preferred_element_type=jnp.float32,
    )


def spread(x, axis, groups):
    n = len(groups[0])
    return lax.all_to_all(
        jnp.broadcast_to(x[None], (n,) + x.shape), axis, 0, 0, tiled=True, axis_index_groups=groups
    )


def flip(x, bits):
    return lax.ppermute(x, "col", [(i, i ^ bits) for i in range(NX * NY)])


def split(x):
    high = x.astype(jnp.bfloat16)
    return high, (x - high.astype(jnp.float32)).astype(jnp.bfloat16)


def dot(a, b):
    return jnp.dot(a, b, preferred_element_type=jnp.float32)


def dot3(a, b):
    return dot(a[0], b[0]) + dot(a[0], b[1]) + dot(a[1], b[0])


def dot3_narrow(a, b):
    both = dot(a[0], jnp.concatenate(b, 1))
    return both[:, :128] + both[:, 128:] + dot(a[1], b[0])


def halves_of(core, own, far):
    return jnp.where(core == 0, own, far), jnp.where(core == 0, far, own)


def squares_kernel(core_ref, own_ref, far_ref, high_ref, low_ref):
    core = core_ref[0]
    squares = []
    for p in range(4):
        order = [COL_GROUPS[0].index(c) for c in range(NX * NY)]
        own = jnp.concatenate([own_ref[i, 8 * p : 8 * p + 8, :] for i in order], 0)
        far = jnp.concatenate([far_ref[i, 8 * p : 8 * p + 8, :] for i in order], 0)
        squares.append(jnp.concatenate(halves_of(core, own, far), 1).T)
    row = lax.broadcasted_iota(jnp.int32, (PW, PW), 0)
    col = lax.broadcasted_iota(jnp.int32, (PW, PW), 1)
    eye = (row == col).astype(jnp.float32)
    power = [split(jnp.where(row > col, x, 0.0)) for x in squares[:2]]
    inverse = [eye - jnp.where(row > col, x, 0.0) for x in squares[:2]]
    for level in range(1, PW.bit_length() - 1):
        cut = 1 << level if level >= 4 else 0

        def square(x):
            full = dot3((x[0][cut:], x[1][cut:]), x)
            return split(jnp.concatenate([jnp.zeros((cut, PW), jnp.float32), full], 0) if cut else full)

        def extend(x, y):
            full = x[cut:] + dot3(split(x[cut:]), y)
            return jnp.concatenate([x[:cut], full], 0) if cut else full

        power = [square(x) for x in power]
        inverse = [extend(x, y) for x, y in zip(inverse, power)]
    for p, x in enumerate(inverse + squares[2:]):
        high, low = split(x)
        high_ref[p] = high
        low_ref[p] = low


def squares_of(core, own, far):
    vmem = pl.BlockSpec(memory_space=pltpu.VMEM)
    pair = jax.ShapeDtypeStruct((4, PW, PW), jnp.bfloat16)
    return pl.pallas_call(
        squares_kernel,
        out_shape=(pair, pair),
        in_specs=[pl.BlockSpec(memory_space=pltpu.SMEM), vmem, vmem],
        out_specs=(vmem, vmem),
        cost_estimate=pl.CostEstimate(flops=6 * 28 * PW**3, bytes_accessed=2 << 20, transcendentals=0),
        compiler_params=pltpu.CompilerParams(vmem_limit_bytes=LIMIT),
        name="squares",
    )(core, own, far)


def update_kernel(
    at_ref, piv_ref, col_ref, local_ref, wide_ref, sq_high_ref, sq_low_ref, block_ref, n0_ref, n1_ref, n2_ref, n3_ref,
    out_ref, near_ref, turned_ref, sems,
):
    me = at_ref[0]
    copies = [
        pltpu.make_async_copy(ref, near_ref.at[bits], sems.at[bits])
        for bits, ref in enumerate((n0_ref, n1_ref, n2_ref, n3_ref))
    ]
    for copy in copies:
        copy.start()

    got = [wide_ref[:, 32 * p : 32 * p + 32, :].reshape(PW, 128) for p in range(2)]
    held = [local_ref[:PW], local_ref[PW:]]
    named = [jnp.broadcast_to(col_ref[:, p : p + 1], (PW, PW)) for p in range(2)]
    again = jnp.logical_and(named[1] == piv_ref[0:1, :], me != 0).astype(jnp.bfloat16)
    twice = dot(again, jnp.concatenate(split(got[0]), 1))
    held[1] = held[1] + twice[:, :128] + twice[:, 128:]
    top = [jnp.where(lax.shift_right_logical(named[p][:, :128], 9) == me, held[p], got[p]) for p in range(2)]

    for bits, copy in enumerate(copies):
        copy.wait()
        x = (at_ref[1] % NX) ^ bits
        for i, y in enumerate(TURN):
            at = pl.multiple_of((NX * y + x) * 8, 8)
            for p in range(2):
                for h in range(4):
                    tile = near_ref[bits, i, 32 * p + 8 * h : 32 * p + 8 * h + 8, :]
                    turned_ref[p, pl.ds(at, 8), 128 * h : 128 * h + 128] = tile
    lower = [split(turned_ref[p].T) for p in range(2)]

    square = [(sq_high_ref[p], sq_low_ref[p]) for p in range(4)]
    upper0 = dot3_narrow(square[0], split(top[0]))
    pair0 = split(upper0)
    upper1 = dot3_narrow(square[1], split(top[1] - dot3_narrow(square[3], pair0)))
    second = got[1] - dot3_narrow(square[2], pair0)
    rank = lax.broadcasted_iota(jnp.int32, (512, PW), 0) + me * 512

    def place(p, x, work):
        select = (rank == piv_ref[p : p + 1, :]).astype(jnp.bfloat16)
        high = x.astype(jnp.bfloat16)
        rest = x - high.astype(jnp.float32)
        mid = rest.astype(jnp.bfloat16)
        low = (rest - mid.astype(jnp.float32)).astype(jnp.bfloat16)
        one = dot(select, jnp.concatenate([high, jnp.ones((PW, 128), jnp.bfloat16)], 1))
        two = dot(select, jnp.concatenate([mid, low], 1))
        moved = one[:, :128] + two[:, :128] + two[:, 128:]
        return jnp.where(one[:, 128:] > 0, moved, work)

    work = place(0, got[0], block_ref[...])
    work = work - dot3_narrow(lower[0], pair0)
    work = place(1, second, work)
    work = work - dot3_narrow(lower[1], split(upper1))
    out_ref[:PW] = jnp.where(me == 0, upper0, work[:PW])
    out_ref[PW:] = jnp.where(me == 0, upper1, work[PW:])


def update_of(at, pivots, local, wide, squares, block, near):
    vmem = pl.BlockSpec(memory_space=pltpu.VMEM)
    return pl.pallas_call(
        update_kernel,
        out_shape=jax.ShapeDtypeStruct((512, 128), jnp.float32),
        in_specs=[pl.BlockSpec(memory_space=pltpu.SMEM)] + [vmem] * 7 + [pl.BlockSpec(memory_space=pl.ANY)] * 4,
        out_specs=vmem,
        scratch_shapes=[
            pltpu.VMEM((NX, NY, 64, 128), jnp.float32),
            pltpu.VMEM((2, PW, 512), jnp.float32),
            pltpu.SemaphoreType.DMA((NX,)),
        ],
        cost_estimate=pl.CostEstimate(flops=1 << 29, bytes_accessed=3 << 20, transcendentals=0),
        compiler_params=pltpu.CompilerParams(vmem_limit_bytes=LIMIT),
        name="update",
    )(at, pivots, pivots.T, local, wide, *squares, block, *near)


def step(block, panels, pivots):
    me = lax.axis_index("row")
    core = me % NC
    start = me * 512
    first = me == 0
    p0, p1 = pivots[0], pivots[1]
    j = jnp.arange(PW, dtype=jnp.int32)
    lane = jnp.arange(512, dtype=jnp.int32)

    def through0(rows):
        hit = p0[None, :] == rows[:, None]
        found = jnp.max(jnp.where(hit, j[None, :], -1), axis=1)
        return jnp.where(found >= 0, found, rows)

    source = jnp.concatenate([p0, through0(p1), j, through0(PW + j)])
    pick = (source[:, None] - start == lane[None, :]).astype(jnp.float32)
    picked = mm(pick, block)
    rows = picked.reshape(2, NC, NZ, 32, 128)
    rows = rows.transpose(1, 2, 0, 3, 4).reshape(NC, NZ, 64, 128)

    pan_t = panels.transpose(0, 2, 1)
    near = pan_t.reshape(2, 8, 4, 128).transpose(0, 2, 1, 3).reshape(64, 128)
    near = spread(near, "col", Y_GROUPS)

    at1 = (p1[:, None] - start == lane[None, :]).astype(jnp.float32)
    piv_t = mm(pan_t[0], at1, 1, 1)
    zero = jnp.zeros((8, PW), jnp.float32)
    own = lambda t: jnp.where(first, t, zero)
    pieces = jnp.stack([own(pan_t[0, :, :PW]), own(pan_t[1, :, PW:]), own(pan_t[0, :, PW:]), piv_t])
    tiles = pieces.reshape(4, 8, 2, 128).transpose(2, 0, 1, 3).reshape(2, 32, 128)

    def side(pair, mine):
        return jnp.where((core == 0) == mine, pair[0], pair[1])

    def halves(mine):
        return jnp.concatenate([side(rows, mine).reshape(512, 128), side(tiles, mine)], 0)

    part = halves(True) + lax.ppermute(halves(False), "row", PAIR)
    part = jnp.concatenate(
        [part[:512].reshape(NZ, 64, 128), jnp.broadcast_to(part[None, 512:], (NZ, 32, 128))], 1
    )
    part, near = lax.optimization_barrier((part, near))

    part = lax.all_to_all(part, "row", 0, 0, tiled=True, axis_index_groups=Z_GROUPS)
    near1 = flip(near, 1)
    part, near, near1 = lax.optimization_barrier((part, near, near1))

    part = jnp.sum(part, 0)
    tile = jnp.broadcast_to(part[64:], (NX * NY, 32, 128))
    tile = lax.all_to_all(tile, "col", 0, 0, tiled=True, axis_index_groups=COL_GROUPS)
    near2 = flip(near, 2)
    far = lax.ppermute(part[:64], "row", PAIR)
    mine = part[:64].reshape(2, 32, 128)
    far = far.reshape(2, 32, 128)
    both = jnp.where(core == 0, jnp.stack([mine, far]), jnp.stack([far, mine]))
    turn = jnp.array(TURN, jnp.int32)
    here = (turn == me // NC)[None, :, None]
    place = jnp.sum(jnp.where(here, pivots.reshape(2, NZ, 32), 0), 1) // 512
    owner = (NC * turn + core)[:, None, None] == place[None]
    wide = jnp.where(owner[..., None], both[None, :, 1], both[None, :, 0]).reshape(NZ, 64, 128)
    tile, wide, near2 = lax.optimization_barrier((tile, wide, near2))

    wide = lax.all_to_all(wide, "row", 0, 0, tiled=True, axis_index_groups=Z_GROUPS)
    far = lax.ppermute(tile, "row", PAIR)
    near3 = flip(near, 3)
    squares = squares_of(core.reshape(1), tile, far)
    wide, squares = lax.optimization_barrier((wide, squares))
    at = jnp.stack([me, lax.axis_index("col")])
    near, near1 = (pltpu.with_memory_space_constraint(x, pltpu.HBM) for x in (near, near1))
    return update_of(at, pivots, picked[:512], wide, squares, block, (near, near1, near2, near3))


def solution(mesh):
    return jax.shard_map(
        step,
        mesh=mesh,
        in_specs=(P("row", "col"), P(None, "row", "col"), P()),
        out_specs=P("row", "col"),
        check_vma=False,
    )
```
